32 devices in a mesh: ctx: 8 (over z, y), fsdp: 4 (over x, core).
Axes of the slice: x: 2, y: 2, z: 4, core: 2. Of those that a mesh axis runs over, the one named last changes fastest.
Arguments:
- queries: bfloat16 [4, 3072, 1024], P('fsdp', 'ctx'), may hold values from -27 to 27
- keys: bfloat16 [4, 3072, 1024], P('fsdp', 'ctx'), may hold values from -27 to 27
- values: bfloat16 [4, 3072, 1024], P('fsdp', 'ctx'), may hold values from -6 to 6
- upstream: bfloat16 [4, 3072, 2048], P('fsdp', 'ctx'), may hold values from -6 to 6
- out_weight: bfloat16 [1024, 2048], P('fsdp'), may hold values from -0.1875 to 0.1875
- slopes: float32 [8], replicated, may hold values from 0.002 to 0.05
- patch_index: int32 [4, 3072], P('fsdp'), may hold values from 0 to 9213, as said below
- pair_lists: int32 [4, 2, 360], P('fsdp', None, 'ctx'), may hold values from 0 to 14, as said below
- pair_counts: int32 [4, 8], P('fsdp', 'ctx'), may hold values from 3 to 45, as said below
Outputs:
- grad_queries: bfloat16 [4, 3072, 1024], P('fsdp', 'ctx')
- grad_keys: bfloat16 [4, 3072, 1024], P('fsdp', 'ctx')
- grad_values: bfloat16 [4, 3072, 1024], P('fsdp', 'ctx')
- grad_out_weight: float32 [1024, 2048], P('fsdp', 'ctx')
The draws below stay inside these ranges and needn't reach their ends.
Inputs may be any that keep to these rules, and one draw needn't show every extreme that they name: `patch_index`: along each folio the numbers rise strictly, by 1 to 3 from one token to the next except before the last token, start at 0 and end at 9213. `pair_lists`: the first pair_counts entries of a device's list are distinct pairs (q, w) with q < 3 and w < 15, in no particular order; every device lists the 3 pairs (q, 6 + q). Entries from the count on are arbitrary pairs of the same ranges and are not attended. `pair_counts`: in every folio some device lists all 45 pairs.
All inputs are finite; a program needn't handle non-finite values.
Results may differ from the reference program's by a relative error of at most 0.015.
Values may be sent and summed in bfloat16 or wider, within the bound.
A program may use at most 192 MiB of HBM per device.

```python
import math
import jax
import jax.numpy as jnp
from jax import lax

D = 2048
HEADS = 8
HDIM = 128
HD = 1024
BLOCK = 128
REACH = 2
GRID = 1024
TOK_DEV = 384
QB = 3
WB = 15
MAXP = 45
SEQ = 3072
N_CTX = 8
N_FSDP = 4


def query_key_draw(key):
    shape = (N_FSDP, SEQ, HD)
    keys_raw = jax.random.truncated_normal(jax.random.fold_in(key, 101), -6.0, 6.0, shape, jnp.float32)
    queries_raw = jax.random.truncated_normal(jax.random.fold_in(key, 102), -6.0, 6.0, shape, jnp.float32)
    return (queries_raw, keys_raw)


def draw_queries(key, part):
    return query_key_draw(key)[0].astype(jnp.bfloat16)


def draw_keys(key, part):
    return query_key_draw(key)[1].astype(jnp.bfloat16)


def draw_patch_index(key, part):
    gaps = jax.random.randint(jax.random.fold_in(key, 201), (N_FSDP, SEQ), 1, 4)
    placed = jnp.cumsum(gaps, axis=1) - gaps[:, :1]
    position = jnp.arange(SEQ)[None, :]
    placed = jnp.where(position == SEQ - 1, 3 * (SEQ - 1), placed)
    return placed.astype(jnp.int32)


def pair_draw(key):
    levels = jax.random.randint(jax.random.fold_in(key, 301), (N_FSDP, N_CTX), 0, 8)
    full_device = jax.random.randint(jax.random.fold_in(key, 302), (N_FSDP,), 0, N_CTX)
    coins = jax.random.randint(jax.random.fold_in(key, 303), (N_FSDP, N_CTX, QB, WB), 0, 8)
    query_ids = jnp.arange(QB)[:, None]
    slot_ids = jnp.arange(WB)[None, :]
    diagonal = slot_ids == query_ids + REACH * QB
    devices = jnp.arange(N_CTX)
    chosen = diagonal[None, None] | (coins < levels[:, :, None, None]) | (devices[None, :, None, None] == full_device[:, None, None, None])
    chosen = chosen.reshape(N_FSDP, N_CTX, MAXP).astype(jnp.int32)
    noise = jax.random.randint(jax.random.fold_in(key, 304), (N_FSDP, N_CTX, MAXP), 0, 2 ** 20)
    order_key = (1 - chosen) * 2 ** 30 + noise * MAXP + jnp.arange(MAXP)[None, None, :]
    ranking = jnp.argsort(order_key, axis=2)
    pair_query = ranking // WB
    pair_slot = ranking % WB
    stacked = jnp.stack([pair_query, pair_slot], axis=1)
    pair_rows = stacked.reshape(N_FSDP, 2, N_CTX * MAXP)
    counts = jnp.sum(chosen, axis=2)
    return (pair_rows.astype(jnp.int32), counts.astype(jnp.int32))


def draw_pair_lists(key, part):
    return pair_draw(key)[0]


def draw_pair_counts(key, part):
    return pair_draw(key)[1]


def spiked(values, stream_key, source, target, blocks, factor):
    def block_of(axis_at):
        return (jnp.arange(values.shape[axis_at]) // (values.shape[axis_at] // blocks)).reshape((-1,) + (1,) * (values.ndim - 1 - axis_at))

    near = jax.random.permutation(stream_key, blocks)[block_of(target)]
    other_side = (block_of(target) + blocks // 2) % blocks
    return jnp.where((block_of(source) == near) | (block_of(source) == other_side), factor * values, values)


def block_scale(key, dims, pieces, least, high):
    gain = 1.0
    for axis_at, parts in pieces:
        draws = jax.random.uniform(jax.random.fold_in(jax.random.fold_in(key, 6), axis_at), (parts,), jnp.float32, least / len(pieces), high / len(pieces))
        gain = gain * jnp.repeat(jnp.exp(draws), dims[axis_at] // parts).reshape((-1,) + (1,) * (len(dims) - 1 - axis_at))
    return gain


def normal_values(rng, extent, width, limit, split=(), kind=jnp.bfloat16):
    factor_of = block_scale(rng, extent, split, -0.22, 0.18) if split else 1.0
    entries = jax.random.normal(rng, extent, jnp.float32) * width * factor_of
    return jnp.minimum(jnp.maximum(entries, -limit), limit).astype(kind)


def bell_draw_with(key, extent, scale, most, shards, heavy, kind=jnp.bfloat16):
    entries = scale * jax.random.normal(key, extent, jnp.float32)
    if shards:
        entries = entries * block_scale(key, extent, shards, -0.22, 0.18)
    return jnp.clip(spiked(entries, jax.random.fold_in(key, 3), *heavy), -most, most).astype(kind)


def setup_inputs(seed: int = 0) -> dict:
    streams_of = jax.random.split(jax.random.key(seed), 10)
    queries = draw_queries(jax.random.fold_in(streams_of[9], 71), 0)
    keys = draw_keys(jax.random.fold_in(streams_of[9], 71), 0)
    values = normal_values(streams_of[2], (N_FSDP, SEQ, HD), 1.0, 6.0, ((0, 4), (1, 8)))
    upstream = bell_draw_with(streams_of[3], (N_FSDP, SEQ, D), 1.0, 6.0, ((0, 4), (1, 8)), (1, 2, 8, 2.0))
    out_weight = normal_values(streams_of[4], (HD, D), HD ** -0.5, 0.1875, ((0, 4),))
    slopes = jnp.clip(jnp.exp(jax.random.uniform(streams_of[5], (HEADS,), jnp.float32, math.log(0.002), math.log(0.05))), 0.002, 0.05)
    patch_index = draw_patch_index(jax.random.fold_in(streams_of[9], 71), 0)
    pair_lists = draw_pair_lists(jax.random.fold_in(streams_of[9], 71), 0)
    pair_counts = draw_pair_counts(jax.random.fold_in(streams_of[9], 71), 0)
    return dict(queries=queries, keys=keys, values=values, upstream=upstream, out_weight=out_weight, slopes=slopes, patch_index=patch_index, pair_lists=pair_lists, pair_counts=pair_counts)


masked_fill = -1e+30

def reference(queries, keys, values, upstream, out_weight, slopes, patch_index, pair_lists, pair_counts):
    scaling = 1.0 / math.sqrt(HDIM)
    out_grad_all = lax.optimization_barrier(jnp.dot(upstream.reshape(N_FSDP * SEQ, D), out_weight.T, preferred_element_type=jnp.float32).astype(jnp.bfloat16)).reshape(N_FSDP, SEQ, HD)
    offsets = jnp.arange(-REACH, REACH + 1, dtype=jnp.int32)
    inside = jnp.arange(TOK_DEV, dtype=jnp.int32)
    pair_ids = jnp.arange(MAXP, dtype=jnp.int32)
    query_ids = jnp.arange(QB, dtype=jnp.int32)
    slot_ids = jnp.arange(WB, dtype=jnp.int32)

    def device_step(running, flat_index):
        key_sums, value_sums = running
        folio_index = (flat_index // N_CTX).astype(jnp.int32)
        device = (flat_index % N_CTX).astype(jnp.int32)
        own_rows = device * TOK_DEV + inside
        owners = (device + offsets) % N_CTX
        window_rows = (owners[:, None] * TOK_DEV + inside[None, :]).reshape(WB * BLOCK)
        query_heads = queries[folio_index][own_rows].astype(jnp.float32).reshape(TOK_DEV, HEADS, HDIM)
        key_heads = keys[folio_index][window_rows].astype(jnp.float32).reshape(WB * BLOCK, HEADS, HDIM)
        value_heads = values[folio_index][window_rows].astype(jnp.float32).reshape(WB * BLOCK, HEADS, HDIM)
        out_grad = out_grad_all[folio_index][own_rows].astype(jnp.float32).reshape(TOK_DEV, HEADS, HDIM)
        positions = patch_index[folio_index]
        query_pos = positions[own_rows]
        key_pos = positions[window_rows]
        distance = (jnp.abs(query_pos[:, None] // GRID - key_pos[None, :] // GRID) + jnp.abs(query_pos[:, None] % GRID - key_pos[None, :] % GRID)).astype(jnp.float32)
        pair_rows = lax.dynamic_slice(pair_lists, (folio_index, jnp.zeros((), jnp.int32), device * MAXP), (1, 2, MAXP))[0]
        listed = pair_ids < pair_counts[folio_index, device]
        block_mask = jnp.any(listed[:, None, None] & (pair_rows[0][:, None, None] == query_ids[None, :, None]) & (pair_rows[1][:, None, None] == slot_ids[None, None, :]), axis=0)
        token_mask = jnp.broadcast_to(block_mask[:, None, :, None], (QB, BLOCK, WB, BLOCK)).reshape(TOK_DEV, WB * BLOCK)
        logits = jnp.einsum('qhd,khd->hqk', query_heads, key_heads) * scaling - slopes[:, None, None] * distance[None]
        logits = jnp.where(token_mask[None], logits, masked_fill)
        row_top = lax.optimization_barrier(jnp.max(logits, axis=2))
        exp_terms = jnp.where(token_mask[None], jnp.exp(logits - row_top[:, :, None]), 0.0)
        row_total = lax.optimization_barrier(jnp.sum(exp_terms, axis=2))
        exp_rounded = lax.optimization_barrier(exp_terms.astype(jnp.bfloat16)).astype(jnp.float32)
        attended = (jnp.einsum('hqk,khd->qhd', exp_rounded, value_heads) / row_total.T[:, :, None]).astype(jnp.bfloat16)
        attended_wide = lax.optimization_barrier(attended).astype(jnp.float32)
        row_delta = lax.optimization_barrier(jnp.sum(out_grad * attended_wide, axis=2)).T
        prob_values = exp_terms / row_total[:, :, None]
        prob_grad = jnp.einsum('qhd,khd->hqk', out_grad, value_heads)
        score_grad = lax.optimization_barrier((prob_values * (prob_grad - row_delta[:, :, None])).astype(jnp.bfloat16)).astype(jnp.float32)
        query_grad = (jnp.einsum('hqk,khd->qhd', score_grad, key_heads) * scaling).astype(jnp.bfloat16)
        key_part = lax.optimization_barrier((jnp.einsum('hqk,qhd->khd', score_grad, query_heads) * scaling).astype(jnp.bfloat16)).astype(jnp.float32)
        prob_rounded = lax.optimization_barrier(prob_values.astype(jnp.bfloat16)).astype(jnp.float32)
        value_part = lax.optimization_barrier(jnp.einsum('hqk,qhd->khd', prob_rounded, out_grad).astype(jnp.bfloat16)).astype(jnp.float32)
        key_sums = key_sums.at[folio_index, window_rows].add(key_part.reshape(WB * BLOCK, HD))
        value_sums = value_sums.at[folio_index, window_rows].add(value_part.reshape(WB * BLOCK, HD))
        return ((key_sums, value_sums), (attended.reshape(TOK_DEV, HD), query_grad.reshape(TOK_DEV, HD)))
    start_sums = (jnp.zeros((N_FSDP, SEQ, HD), jnp.float32), jnp.zeros((N_FSDP, SEQ, HD), jnp.float32))
    (key_sums, value_sums), (attended_all, query_all) = lax.scan(device_step, start_sums, jnp.arange(N_FSDP * N_CTX, dtype=jnp.int32))
    attended_all = attended_all.reshape(N_FSDP * SEQ, HD)
    grad_queries = query_all.reshape(N_FSDP, SEQ, HD)
    weight_grad = jnp.dot(attended_all.T, upstream.reshape(N_FSDP * SEQ, D), preferred_element_type=jnp.float32) / math.sqrt(N_FSDP * SEQ)
    return (grad_queries, key_sums.astype(jnp.bfloat16), value_sums.astype(jnp.bfloat16), weight_grad)
```

```python
import functools
import math

import jax
import jax.numpy as jnp
from jax import lax
from jax.experimental import pallas as pl
from jax.experimental.pallas import tpu as pltpu
from jax.sharding import PartitionSpec as P

BLOCK = 128
REACH = 2
GRID = 1024
FAR = 1e32
CHUNKS = 2
MESH = pl.DeviceIdType.MESH
F32 = jnp.float32
BF16 = jnp.bfloat16


def nt(a, b):
    return lax.dot_general(a, b, (((1,), (1,)), ((), ())), preferred_element_type=F32)


def nn(a, b):
    return lax.dot_general(a, b, (((1,), (0,)), ((), ())), preferred_element_type=F32)


def tn(a, b):
    return lax.dot_general(a, b, (((0,), (0,)), ((), ())), preferred_element_type=F32)


def greet(targets):
    barrier = pltpu.get_barrier_semaphore()
    for target in targets:
        pl.semaphore_signal(barrier, inc=1, device_id=target, device_id_type=MESH)
    pl.semaphore_wait(barrier, len(targets))


class Gather:
    def __init__(self, pieces, send_sem, recv_sem):
        n = lax.axis_size("ctx")
        me = lax.axis_index("ctx")
        self.parity = lax.rem(me, 2)
        self.up = lax.rem(me + 2, n)
        self.down = lax.rem(me + n - 2, n)
        self.partner = me + 1 - 2 * self.parity
        self.pieces = pieces
        self.send_sem = send_sem
        self.recv_sem = recv_sem

    def targets(self):
        return [{"ctx": self.up}, {"ctx": self.down}, {"ctx": self.partner}]

    def copy(self, i, slot):
        own, land = self.pieces[i]
        src = land(1 - self.parity) if slot == 3 else own
        target = (self.up, self.down, self.partner, self.partner)[slot]
        return pltpu.make_async_remote_copy(
            src_ref=src,
            dst_ref=land(slot),
            send_sem=self.send_sem.at[i, slot],
            recv_sem=self.recv_sem.at[i, slot],
            device_id={"ctx": target},
            device_id_type=MESH,
        )

    def start(self):
        for i in range(len(self.pieces)):
            for slot in (0, 1, 2):
                self.copy(i, slot).start()

    def relay(self, i):
        src = 1 - self.parity
        own, land = self.pieces[i]
        pltpu.make_async_remote_copy(
            src_ref=own,
            dst_ref=land(src),
            send_sem=self.send_sem.at[i, 0],
            recv_sem=self.recv_sem.at[i, src],
            device_id={"ctx": self.partner},
            device_id_type=MESH,
        ).wait_recv()
        self.copy(i, 3).start()

    def arrived(self, slot):
        for i in range(len(self.pieces)):
            own, land = self.pieces[i]
            pltpu.make_async_remote_copy(
                src_ref=own,
                dst_ref=land(slot),
                send_sem=self.send_sem.at[i, 0],
                recv_sem=self.recv_sem.at[i, slot],
                device_id={"ctx": self.partner},
                device_id_type=MESH,
            ).wait_recv()

    def sent(self):
        for i in range(len(self.pieces)):
            for slot in range(4):
                self.copy(i, slot).wait_send()


def row_pieces(own_ref, land_ref, index, chunks):
    rows = own_ref.shape[0] // chunks

    def piece(j):
        span = pl.ds(j * rows, rows)

        def land(slot):
            return land_ref.at[slot, index, span] if index is not None else land_ref.at[slot, span]

        return (own_ref.at[span], land)

    return [piece(j) for j in range(chunks)]


def build_distance(far_ref, wrow_ref, wcol_ref, key_at, query_at, mask_row, tokens):
    qs = pl.ds(pl.multiple_of(query_at * tokens, BLOCK), tokens)
    qr = wrow_ref[0:1, qs]
    qg = wrow_ref[1:2, qs]
    for b in range(tokens // BLOCK):
        ks = pl.ds(pl.multiple_of(key_at * tokens + b * BLOCK, BLOCK), BLOCK)
        kc = wcol_ref[ks, :]
        dist = jnp.abs(kc[:, 0:1] - qr) + jnp.abs(kc[:, 1:2] - qg)
        far_ref[b * BLOCK : (b + 1) * BLOCK, :] = jnp.where(mask_row(b) > 0.5, dist, FAR)


def head_span(h, size):
    return pl.ds(pl.multiple_of(h * size, size), size)


def forward_kernel(
    heads,
    slopes_ref,
    q_ref,
    k_ref,
    v_ref,
    up_ref,
    w_ref,
    wrow_ref,
    wcol_ref,
    mask_ref,
    kv_ref,
    og_ref,
    att_ref,
    stats_ref,
    wbuf_ref,
    far_ref,
    top_ref,
    total_ref,
    acc_ref,
    send_sem,
    recv_sem,
    wsend_sem,
    wrecv_sem,
):
    tokens, width = q_ref.shape
    size = width // heads
    blocks = tokens // BLOCK
    scaling = 1.0 / math.sqrt(size)
    nf = lax.axis_size("fsdp")
    fs = lax.axis_index("fsdp")
    wrows = w_ref.shape[0]
    gather = Gather(
        row_pieces(k_ref, kv_ref, 0, CHUNKS) + row_pieces(v_ref, kv_ref, 1, CHUNKS),
        send_sem,
        recv_sem,
    )
    greet(gather.targets() + [{"fsdp": lax.rem(fs + d, nf)} for d in range(1, nf)])
    gather.start()
    wcopies = [
        pltpu.make_async_remote_copy(
            src_ref=w_ref,
            dst_ref=wbuf_ref.at[d - 1],
            send_sem=wsend_sem.at[d - 1],
            recv_sem=wrecv_sem.at[d - 1],
            device_id={"fsdp": lax.rem(fs + d, nf)},
            device_id_type=MESH,
        )
        for d in range(1, nf)
    ]
    for copy in wcopies:
        copy.start()

    top_ref[...] = jnp.full(top_ref.shape, -1e30, F32)
    total_ref[...] = jnp.zeros(total_ref.shape, F32)
    acc_ref[...] = jnp.zeros(acc_ref.shape, F32)

    def visit(keys, values, offset):
        at = offset + REACH

        def mask_row(b):
            return mask_ref[pl.ds(at * blocks + b, 1), :]

        build_distance(far_ref, wrow_ref, wcol_ref, at, REACH, mask_row, tokens)

        @pl.loop(0, heads)
        def _(h):
            hs = head_span(h, size)
            s = nt(keys[:, hs], q_ref[:, hs]) * scaling - slopes_ref[h] * far_ref[...]
            old = top_ref[h]
            new = jnp.maximum(old, jnp.max(s, axis=0, keepdims=True))
            factor = jnp.exp(old - new)
            p = jnp.exp(s - new)
            top_ref[h] = new
            total_ref[h] = total_ref[h] * factor + jnp.sum(p, axis=0, keepdims=True)
            acc_ref[h] = acc_ref[h] * factor + tn(values[:, hs], p.astype(BF16))

    def visit_slot(slot, offset):
        visit(kv_ref.at[slot, 0], kv_ref.at[slot, 1], offset)

    def project(block, owner):
        cols = pl.ds(pl.multiple_of(owner * wrows, BLOCK), wrows)
        og_ref[:, cols] = nt(up_ref[...], block[...]).astype(BF16)

    parity = gather.parity
    near = 1 - 2 * parity
    visit(k_ref, v_ref, 0)
    project(w_ref, fs)
    for i in range(len(gather.pieces)):
        gather.relay(i)
    visit_slot(1 - parity, 2 * near)
    gather.arrived(2)
    visit_slot(2, near)
    for d in range(1, nf):
        wcopies[d - 1].wait()
        project(wbuf_ref.at[d - 1], lax.rem(fs + nf - d, nf))
    gather.arrived(parity)
    visit_slot(parity, -2 * near)
    gather.arrived(3)
    visit_slot(3, -near)
    for h in range(heads):
        hs = slice(h * size, (h + 1) * size)
        total = total_ref[h]
        att_t = acc_ref[h] / total
        att = att_t.T.astype(BF16)
        att_ref[:, hs] = att
        stats_ref[h : h + 1, :] = top_ref[h] + jnp.log(total)
        prod = og_ref[:, hs].astype(F32) * att.astype(F32)
        stats_ref[heads + h : heads + h + 1, :] = jnp.sum(prod.T, axis=0, keepdims=True)
    stats_ref[2 * heads :, :] = mask_ref[...]
    gather.sent()


def backward_kernel(
    heads,
    slopes_ref,
    q_ref,
    k_ref,
    v_ref,
    og_ref,
    stats_ref,
    kv_ref,
    wrow_ref,
    wcol_ref,
    dq_ref,
    dk_ref,
    dv_ref,
    qbuf_ref,
    obuf_ref,
    sbuf_ref,
    far_ref,
    dqt_ref,
    dka_ref,
    dva_ref,
    send_sem,
    recv_sem,
):
    tokens, width = q_ref.shape
    size = width // heads
    blocks = tokens // BLOCK
    scaling = 1.0 / math.sqrt(size)
    gather = Gather(
        row_pieces(stats_ref, sbuf_ref, None, 1)
        + row_pieces(q_ref, qbuf_ref, None, CHUNKS)
        + row_pieces(og_ref, obuf_ref, None, CHUNKS),
        send_sem,
        recv_sem,
    )
    greet(gather.targets())
    gather.start()

    def visit(keys, values, queries, grads, stats, key_at, query_at, to_query, to_key, first):
        def mask_row(b):
            return stats[pl.ds(2 * heads + (key_at - query_at + REACH) * blocks + b, 1), :]

        build_distance(far_ref, wrow_ref, wcol_ref, key_at, query_at, mask_row, tokens)

        @pl.loop(0, heads)
        def _(h):
            hs = head_span(h, size)
            k, q, g = keys[:, hs], queries[:, hs], grads[:, hs]
            s = nt(k, q) * scaling - slopes_ref[h] * far_ref[...]
            p = jnp.exp(s - stats[pl.ds(h, 1), :])
            ds = (p * (nt(values[:, hs], g) - stats[pl.ds(heads + h, 1), :])).astype(BF16)
            if to_query:
                part = tn(k, ds)
                dqt_ref[h] = part if first else dqt_ref[h] + part
            if to_key:
                kpart = nn(ds, q)
                vpart = nn(p.astype(BF16), g)
                dka_ref[h] = kpart if first else dka_ref[h] + kpart
                dva_ref[h] = vpart if first else dva_ref[h] + vpart

    parity = gather.parity
    near = 1 - 2 * parity
    home = REACH

    def to_query(slot, offset):
        visit(
            kv_ref.at[slot, 0], kv_ref.at[slot, 1], q_ref, og_ref, stats_ref,
            home + offset, home, True, False, False,
        )

    def to_key(slot, offset):
        visit(
            k_ref, v_ref, qbuf_ref.at[slot], obuf_ref.at[slot], sbuf_ref.at[slot],
            home, home + offset, False, True, False,
        )

    visit(k_ref, v_ref, q_ref, og_ref, stats_ref, home, home, True, True, True)
    to_query(0, -2)
    to_query(1, 2)
    for i in range(1 + CHUNKS):
        gather.relay(i)
    to_query(2, near)
    for i in range(1 + CHUNKS, len(gather.pieces)):
        gather.relay(i)
    to_query(3, -near)
    for h in range(heads):
        dq_ref[:, h * size : (h + 1) * size] = (dqt_ref[h].T * scaling).astype(BF16)
    to_key(1 - parity, 2 * near)
    gather.arrived(2)
    to_key(2, near)
    gather.arrived(parity)
    to_key(parity, -2 * near)
    gather.arrived(3)
    to_key(3, -near)
    for h in range(heads):
        hs = slice(h * size, (h + 1) * size)
        dk_ref[:, hs] = (dka_ref[h] * scaling).astype(BF16)
        dv_ref[:, hs] = dva_ref[h].astype(BF16)
    gather.sent()


def on_device(
    queries, keys, values, upstream, out_weight, slopes, patch_index, pair_lists, pair_counts
):
    n = lax.axis_size("ctx")
    nf = lax.axis_size("fsdp")
    me = lax.axis_index("ctx")
    tokens, width = queries.shape[1:]
    model = upstream.shape[2]
    heads = slopes.shape[0]
    size = width // heads
    blocks = tokens // BLOCK
    window = 2 * REACH + 1
    slots = window * blocks
    mask_rows = -(-slots // 8) * 8

    positions = patch_index[0]
    around = lax.dynamic_slice_in_dim(
        jnp.concatenate([positions, positions]), lax.rem(me + n - REACH, n) * tokens, window * tokens
    )
    rows_cols = jnp.stack([around // GRID, around % GRID]).astype(F32)
    wrow = jnp.pad(rows_cols, ((0, 6), (0, 0)))
    wcol = wrow.T
    pairs = pair_lists[0]
    listed = jnp.arange(pairs.shape[1]) < pair_counts[0, 0]
    hit = (
        listed[None, None, :]
        & (pairs[0][None, None, :] == jnp.arange(blocks)[None, :, None])
        & (pairs[1][None, None, :] == jnp.arange(mask_rows)[:, None, None])
    )
    block_mask = jnp.any(hit, axis=2).astype(F32)
    mask = jnp.broadcast_to(block_mask[:, :, None], (mask_rows, blocks, BLOCK)).reshape(
        mask_rows, tokens
    )

    vmem = pl.BlockSpec(memory_space=pltpu.VMEM)
    smem = pl.BlockSpec(memory_space=pltpu.SMEM)
    block = jax.ShapeDtypeStruct((tokens, width), BF16)
    q, k, v = queries[0], keys[0], values[0]
    pair_flops = 2 * tokens * tokens * window * width
    stat_rows = 2 * heads + mask_rows
    pieces = 2 * CHUNKS
    kv, og, att, stats = pl.pallas_call(
        functools.partial(forward_kernel, heads),
        out_shape=(
            jax.ShapeDtypeStruct((4, 2, tokens, width), BF16),
            block,
            block,
            jax.ShapeDtypeStruct((stat_rows, tokens), F32),
        ),
        in_specs=[smem] + [vmem] * 8,
        out_specs=(vmem,) * 4,
        scratch_shapes=[
            pltpu.VMEM((nf - 1,) + out_weight.shape, BF16),
            pltpu.VMEM((tokens, tokens), F32),
            pltpu.VMEM((heads, 1, tokens), F32),
            pltpu.VMEM((heads, 1, tokens), F32),
            pltpu.VMEM((heads, size, tokens), F32),
            pltpu.SemaphoreType.DMA((pieces, 4)),
            pltpu.SemaphoreType.DMA((pieces, 4)),
            pltpu.SemaphoreType.DMA((nf - 1,)),
            pltpu.SemaphoreType.DMA((nf - 1,)),
        ],
        compiler_params=pltpu.CompilerParams(
            collective_id=0, has_side_effects=True, vmem_limit_bytes=48 * 2**20
        ),
        cost_estimate=pl.CostEstimate(
            flops=2 * pair_flops, bytes_accessed=100 * 2**20, transcendentals=0
        ),
        name="forward",
    )(slopes, q, k, v, upstream[0], out_weight, wrow, wcol, mask)

    partial = (
        lax.dot_general(att, upstream[0], (((0,), (0,)), ((), ())), preferred_element_type=F32)
        .astype(BF16)
        .reshape(nf, width // nf, n, model // n)
        .transpose(0, 2, 1, 3)
        .reshape(nf * n, width // nf, model // n)
    )
    weight_grad = lax.psum_scatter(
        partial, ("fsdp", "ctx"), scatter_dimension=0, tiled=False
    ).astype(F32) / math.sqrt(tokens * n * nf)

    pieces = 2 * CHUNKS + 1
    dq, dk, dv = pl.pallas_call(
        functools.partial(backward_kernel, heads),
        out_shape=(block,) * 3,
        in_specs=[smem] + [vmem] * 8,
        out_specs=(vmem,) * 3,
        scratch_shapes=[
            pltpu.VMEM((4, tokens, width), BF16),
            pltpu.VMEM((4, tokens, width), BF16),
            pltpu.VMEM((4, stat_rows, tokens), F32),
            pltpu.VMEM((tokens, tokens), F32),
            pltpu.VMEM((heads, size, tokens), F32),
            pltpu.VMEM((heads, tokens, size), F32),
            pltpu.VMEM((heads, tokens, size), F32),
            pltpu.SemaphoreType.DMA((pieces, 4)),
            pltpu.SemaphoreType.DMA((pieces, 4)),
        ],
        compiler_params=pltpu.CompilerParams(
            collective_id=1, has_side_effects=True, vmem_limit_bytes=48 * 2**20
        ),
        cost_estimate=pl.CostEstimate(
            flops=8 * pair_flops, bytes_accessed=300 * 2**20, transcendentals=0
        ),
        name="backward",
    )(slopes, q, k, v, og, stats, kv, wrow, wcol)
    return (dq[None], dk[None], dv[None], weight_grad)


def solution(mesh):
    in_specs = (
        P("fsdp", "ctx", None),
        P("fsdp", "ctx", None),
        P("fsdp", "ctx", None),
        P("fsdp", "ctx", None),
        P("fsdp", None),
        P(),
        P("fsdp", None),
        P("fsdp", None, "ctx"),
        P("fsdp", "ctx"),
    )
    out_specs = (
        P("fsdp", "ctx", None),
        P("fsdp", "ctx", None),
        P("fsdp", "ctx", None),
        P("fsdp", "ctx"),
    )
    return jax.shard_map(
        on_device, mesh=mesh, in_specs=in_specs, out_specs=out_specs, check_vma=False
    )
```

```python
import functools
import math

import jax
import jax.numpy as jnp
from jax import lax
from jax.experimental import pallas as pl
from jax.experimental.pallas import tpu as pltpu
from jax.sharding import PartitionSpec as P

BLOCK = 128
REACH = 2
GRID = 1024
FAR = 1e32
CHUNKS = 2
MESH = pl.DeviceIdType.MESH
F32 = jnp.float32
BF16 = jnp.bfloat16


def nt(a, b):
    return lax.dot_general(a, b, (((1,), (1,)), ((), ())), preferred_element_type=F32)


def nn(a, b):
    return lax.dot_general(a, b, (((1,), (0,)), ((), ())), preferred_element_type=F32)


def tn(a, b):
    return lax.dot_general(a, b, (((0,), (0,)), ((), ())), preferred_element_type=F32)


def greet(targets):
    barrier = pltpu.get_barrier_semaphore()
    for target in targets:
        pl.semaphore_signal(barrier, inc=1, device_id=target, device_id_type=MESH)
    pl.semaphore_wait(barrier, len(targets))


class Gather:
    def __init__(self, pieces, send_sem, recv_sem):
        n = lax.axis_size("ctx")
        me = lax.axis_index("ctx")
        self.parity = lax.rem(me, 2)
        self.up = lax.rem(me + 2, n)
        self.down = lax.rem(me + n - 2, n)
        self.partner = me + 1 - 2 * self.parity
        self.pieces = pieces
        self.send_sem = send_sem
        self.recv_sem = recv_sem

    def copy(self, i, slot):
        own, land = self.pieces[i]
        src = land(1 - self.parity) if slot == 3 else own
        target = (self.up, self.down, self.partner, self.partner)[slot]
        return pltpu.make_async_remote_copy(
            src_ref=src,
            dst_ref=land(slot),
            send_sem=self.send_sem.at[i, slot],
            recv_sem=self.recv_sem.at[i, slot],
            device_id={"ctx": target},
            device_id_type=MESH,
        )

    def start(self, pieces):
        for i in pieces:
            for slot in (0, 1, 2):
                self.copy(i, slot).start()

    def relay(self, i):
        src = 1 - self.parity
        own, land = self.pieces[i]
        pltpu.make_async_remote_copy(
            src_ref=own,
            dst_ref=land(src),
            send_sem=self.send_sem.at[i, 0],
            recv_sem=self.recv_sem.at[i, src],
            device_id={"ctx": self.partner},
            device_id_type=MESH,
        ).wait_recv()
        self.copy(i, 3).start()

    def arrived(self, slot, pieces):
        for i in pieces:
            own, land = self.pieces[i]
            pltpu.make_async_remote_copy(
                src_ref=own,
                dst_ref=land(slot),
                send_sem=self.send_sem.at[i, 0],
                recv_sem=self.recv_sem.at[i, slot],
                device_id={"ctx": self.partner},
                device_id_type=MESH,
            ).wait_recv()

    def sent(self):
        for i in range(len(self.pieces)):
            for slot in range(4):
                self.copy(i, slot).wait_send()


def remote(src, dst, send_sem, recv_sem, target):
    return pltpu.make_async_remote_copy(
        src_ref=src, dst_ref=dst, send_sem=send_sem, recv_sem=recv_sem, device_id=target, device_id_type=MESH
    )


def row_pieces(own_ref, land_ref, index, chunks):
    rows = own_ref.shape[0] // chunks

    def piece(j):
        span = pl.ds(j * rows, rows)

        def land(slot):
            return land_ref.at[slot, index, span] if index is not None else land_ref.at[slot, span]

        return (own_ref.at[span], land)

    return [piece(j) for j in range(chunks)]


def build_distance(far_ref, wrow_ref, wcol_ref, key_at, query_at, mask_row, tokens):
    qs = pl.ds(pl.multiple_of(query_at * tokens, BLOCK), tokens)
    qr = wrow_ref[0:1, qs]
    qg = wrow_ref[1:2, qs]
    for b in range(tokens // BLOCK):
        ks = pl.ds(pl.multiple_of(key_at * tokens + b * BLOCK, BLOCK), BLOCK)
        kc = wcol_ref[ks, :]
        dist = jnp.abs(kc[:, 0:1] - qr) + jnp.abs(kc[:, 1:2] - qg)
        far_ref[b * BLOCK : (b + 1) * BLOCK, :] = jnp.where(mask_row(b) > 0.5, dist, FAR)


def head_span(h, size):
    return pl.ds(pl.multiple_of(h * size, size), size)


def fused_kernel(
    heads,
    weight_scale,
    slopes_ref,
    q_ref,
    k_ref,
    v_ref,
    up_ref,
    w_ref,
    wrow_ref,
    wcol_ref,
    mask_ref,
    dq_ref,
    dk_ref,
    dv_ref,
    wg_ref,
    kv_ref,
    qbuf_ref,
    obuf_ref,
    sbuf_ref,
    og_ref,
    att_ref,
    stats_ref,
    wbuf_ref,
    far_ref,
    top_ref,
    total_ref,
    acc_ref,
    dka_ref,
    dva_ref,
    part_ref,
    pland_ref,
    wsum_ref,
    ysum_ref,
    zland_ref,
    send_sem,
    recv_sem,
    wsend_sem,
    wrecv_sem,
    gsend_sem,
    grecv_sem,
    ysem,
    zsend_sem,
    zrecv_sem,
):
    tokens, width = q_ref.shape
    size = width // heads
    blocks = tokens // BLOCK
    scaling = 1.0 / math.sqrt(size)
    n = lax.axis_size("ctx")
    nf = lax.axis_size("fsdp")
    me = lax.axis_index("ctx")
    fs = lax.axis_index("fsdp")
    wrows = w_ref.shape[0]
    model = up_ref.shape[1]
    half = n // 2
    wide = wsum_ref.shape[3]
    kv_pieces = range(0, 2 * CHUNKS)
    q_pieces = range(2 * CHUNKS, 3 * CHUNKS)
    o_pieces = range(3 * CHUNKS, 4 * CHUNKS)
    s_pieces = range(4 * CHUNKS, 4 * CHUNKS + 1)
    late_pieces = range(2 * CHUNKS, 4 * CHUNKS + 1)
    gather = Gather(
        row_pieces(k_ref, kv_ref, 0, CHUNKS)
        + row_pieces(v_ref, kv_ref, 1, CHUNKS)
        + row_pieces(q_ref, qbuf_ref, None, CHUNKS)
        + row_pieces(og_ref, obuf_ref, None, CHUNKS)
        + row_pieces(stats_ref, sbuf_ref, None, 1),
        send_sem,
        recv_sem,
    )
    parity = gather.parity
    near = 1 - 2 * parity
    home = REACH
    others = [{"fsdp": lax.rem(fs + d, nf)} for d in range(1, nf)]
    across = [{"ctx": lax.rem(me + 2 * d, n)} for d in range(1, half)]
    greet([{"ctx": gather.partner}] + across + others)
    gather.start(kv_pieces)
    wcopies = [
        remote(w_ref, wbuf_ref.at[d - 1], wsend_sem.at[d - 1], wrecv_sem.at[d - 1], others[d - 1])
        for d in range(1, nf)
    ]
    for copy in wcopies:
        copy.start()

    top_ref[...] = jnp.full(top_ref.shape, -1e30, F32)
    total_ref[...] = jnp.zeros(total_ref.shape, F32)
    acc_ref[...] = jnp.zeros(acc_ref.shape, F32)

    def look(keys, values, offset):
        at = offset + REACH

        def mask_row(b):
            return mask_ref[pl.ds(at * blocks + b, 1), :]

        build_distance(far_ref, wrow_ref, wcol_ref, at, home, mask_row, tokens)

        @pl.loop(0, heads)
        def _(h):
            hs = head_span(h, size)
            s = nt(keys[:, hs], q_ref[:, hs]) * scaling - slopes_ref[h] * far_ref[...]
            old = top_ref[h]
            new = jnp.maximum(old, jnp.max(s, axis=0, keepdims=True))
            factor = jnp.exp(old - new)
            p = jnp.exp(s - new)
            top_ref[h] = new
            total_ref[h] = total_ref[h] * factor + jnp.sum(p, axis=0, keepdims=True)
            acc_ref[h] = acc_ref[h] * factor + tn(values[:, hs], p.astype(BF16))

    def look_slot(slot, offset):
        look(kv_ref.at[slot, 0], kv_ref.at[slot, 1], offset)

    def project(block, owner):
        cols = pl.ds(pl.multiple_of(owner * wrows, BLOCK), wrows)
        og_ref[:, cols] = nt(up_ref[...], block[...]).astype(BF16)

    look(k_ref, v_ref, 0)
    project(w_ref, fs)
    for i in kv_pieces:
        gather.relay(i)
    gather.start(q_pieces)
    look_slot(1 - parity, 2 * near)
    for d in range(1, nf):
        wcopies[d - 1].wait()
        project(wbuf_ref.at[d - 1], lax.rem(fs + nf - d, nf))
    gather.start(o_pieces)
    gather.arrived(2, kv_pieces)
    look_slot(2, near)
    gather.arrived(parity, kv_pieces)
    look_slot(parity, -2 * near)
    gather.arrived(3, kv_pieces)
    look_slot(3, -near)
    for h in range(heads):
        hs = slice(h * size, (h + 1) * size)
        total = total_ref[h]
        att = (acc_ref[h] / total).T.astype(BF16)
        att_ref[:, hs] = att
        stats_ref[h : h + 1, :] = top_ref[h] + jnp.log(total)
        prod = og_ref[:, hs].astype(F32) * att.astype(F32)
        stats_ref[heads + h : heads + h + 1, :] = jnp.sum(prod.T, axis=0, keepdims=True)
    stats_ref[2 * heads :, :] = mask_ref[...]
    gather.start(s_pieces)

    gcopies = []
    for d in range(1, nf):
        owner = lax.rem(fs + d, nf)
        cols = pl.ds(pl.multiple_of(owner * wrows, BLOCK), wrows)
        part_ref[d - 1] = tn(att_ref[:, cols], up_ref[...]).astype(BF16)
        copy = remote(
            part_ref.at[d - 1], pland_ref.at[d - 1], gsend_sem.at[d - 1], grecv_sem.at[d - 1], others[d - 1]
        )
        copy.start()
        gcopies.append(copy)

    def visit(keys, values, queries, grads, stats, key_at, query_at, to_query, to_key, first):
        def mask_row(b):
            return stats[pl.ds(2 * heads + (key_at - query_at + REACH) * blocks + b, 1), :]

        build_distance(far_ref, wrow_ref, wcol_ref, key_at, query_at, mask_row, tokens)

        @pl.loop(0, heads)
        def _(h):
            hs = head_span(h, size)
            k, q, g = keys[:, hs], queries[:, hs], grads[:, hs]
            s = nt(k, q) * scaling - slopes_ref[h] * far_ref[...]
            p = jnp.exp(s - stats[pl.ds(h, 1), :])
            ds = (p * (nt(values[:, hs], g) - stats[pl.ds(heads + h, 1), :])).astype(BF16)
            if to_query:
                part = tn(k, ds)
                acc_ref[h] = part if first else acc_ref[h] + part
            if to_key:
                kpart = nn(ds, q)
                vpart = nn(p.astype(BF16), g)
                dka_ref[h] = kpart if first else dka_ref[h] + kpart
                dva_ref[h] = vpart if first else dva_ref[h] + vpart

    def to_query(slot, offset):
        visit(
            kv_ref.at[slot, 0], kv_ref.at[slot, 1], q_ref, og_ref, stats_ref,
            home + offset, home, True, False, False,
        )

    def to_key(slot, offset):
        visit(
            k_ref, v_ref, qbuf_ref.at[slot], obuf_ref.at[slot], sbuf_ref.at[slot],
            home, home + offset, False, True, False,
        )

    for i in q_pieces:
        gather.relay(i)
    visit(k_ref, v_ref, q_ref, og_ref, stats_ref, home, home, True, True, True)
    to_query(0, -2)
    for i in o_pieces:
        gather.relay(i)
    to_query(1, 2)
    for i in s_pieces:
        gather.relay(i)
    to_query(2, near)
    to_query(3, -near)
    for h in range(heads):
        dq_ref[:, h * size : (h + 1) * size] = (acc_ref[h].T * scaling).astype(BF16)

    mine = tn(att_ref[:, pl.ds(pl.multiple_of(fs * wrows, BLOCK), wrows)], up_ref[...])
    for copy in gcopies:
        copy.wait()
    for d in range(1, nf):
        mine = mine + pland_ref[d - 1].astype(F32)
    for c in range(n):
        at = c * (model // n) // wide * wide
        wsum_ref[c % 2, c // 2] = mine[:, at : at + wide].astype(BF16)
    ycopy = remote(
        wsum_ref.at[1 - parity], ysum_ref, ysem.at[0], ysem.at[1], {"ctx": gather.partner}
    )
    ycopy.start()

    to_key(1 - parity, 2 * near)
    gather.arrived(2, late_pieces)
    to_key(2, near)

    ycopy.wait()
    row = lax.div(me, 2)
    zcopies = []
    for d in range(half):
        k = lax.rem(row + d, half)
        pair_sum = wsum_ref[parity, k].astype(F32) + ysum_ref[k].astype(F32)
        if d == 0:
            wg_ref[...] = pair_sum
            continue
        zland_ref[0, d - 1] = pair_sum.astype(BF16)
        copy = remote(
            zland_ref.at[0, d - 1], zland_ref.at[1, d - 1], zsend_sem.at[d - 1], zrecv_sem.at[d - 1], across[d - 1]
        )
        copy.start()
        zcopies.append(copy)

    gather.arrived(parity, late_pieces)
    to_key(parity, -2 * near)
    gather.arrived(3, late_pieces)
    to_key(3, -near)
    for h in range(heads):
        hs = slice(h * size, (h + 1) * size)
        dk_ref[:, hs] = (dka_ref[h] * scaling).astype(BF16)
        dv_ref[:, hs] = dva_ref[h].astype(BF16)
    total = wg_ref[...]
    for d in range(1, half):
        zcopies[d - 1].wait()
        total = total + zland_ref[1, d - 1].astype(F32)
    wg_ref[...] = total * weight_scale
    gather.sent()


def on_device(
    queries, keys, values, upstream, out_weight, slopes, patch_index, pair_lists, pair_counts
):
    n = lax.axis_size("ctx")
    nf = lax.axis_size("fsdp")
    me = lax.axis_index("ctx")
    tokens, width = queries.shape[1:]
    model = upstream.shape[2]
    heads = slopes.shape[0]
    size = width // heads
    blocks = tokens // BLOCK
    window = 2 * REACH + 1
    slots = window * blocks
    mask_rows = -(-slots // 8) * 8

    positions = patch_index[0]
    around = lax.dynamic_slice_in_dim(
        jnp.concatenate([positions, positions]), lax.rem(me + n - REACH, n) * tokens, window * tokens
    )
    rows_cols = jnp.stack([around // GRID, around % GRID]).astype(F32)
    wrow = jnp.pad(rows_cols, ((0, 6), (0, 0)))
    wcol = wrow.T
    pairs = pair_lists[0]
    listed = jnp.arange(pairs.shape[1]) < pair_counts[0, 0]
    hit = (
        listed[None, None, :]
        & (pairs[0][None, None, :] == jnp.arange(blocks)[None, :, None])
        & (pairs[1][None, None, :] == jnp.arange(mask_rows)[:, None, None])
    )
    block_mask = jnp.any(hit, axis=2).astype(F32)
    mask = jnp.broadcast_to(block_mask[:, :, None], (mask_rows, blocks, BLOCK)).reshape(
        mask_rows, tokens
    )

    vmem = pl.BlockSpec(memory_space=pltpu.VMEM)
    smem = pl.BlockSpec(memory_space=pltpu.SMEM)
    block = jax.ShapeDtypeStruct((tokens, width), BF16)
    pair_flops = 2 * tokens * tokens * window * width
    stat_rows = 2 * heads + mask_rows
    pieces = 4 * CHUNKS + 1
    wrows = out_weight.shape[0]
    cut = model // n
    wide = max(cut, BLOCK)
    half = n // 2
    dq, dk, dv, weight_grad = pl.pallas_call(
        functools.partial(fused_kernel, heads, 1.0 / math.sqrt(tokens * n * nf)),
        out_shape=(block, block, block, jax.ShapeDtypeStruct((wrows, wide), F32)),
        in_specs=[smem] + [vmem] * 8,
        out_specs=(vmem,) * 4,
        scratch_shapes=[
            pltpu.VMEM((4, 2, tokens, width), BF16),
            pltpu.VMEM((4, tokens, width), BF16),
            pltpu.VMEM((4, tokens, width), BF16),
            pltpu.VMEM((4, stat_rows, tokens), F32),
            pltpu.VMEM((tokens, width), BF16),
            pltpu.VMEM((tokens, width), BF16),
            pltpu.VMEM((stat_rows, tokens), F32),
            pltpu.VMEM((nf - 1,) + out_weight.shape, BF16),
            pltpu.VMEM((tokens, tokens), F32),
            pltpu.VMEM((heads, 1, tokens), F32),
            pltpu.VMEM((heads, 1, tokens), F32),
            pltpu.VMEM((heads, size, tokens), F32),
            pltpu.VMEM((heads, tokens, size), F32),
            pltpu.VMEM((heads, tokens, size), F32),
            pltpu.VMEM((nf - 1, wrows, model), BF16),
            pltpu.VMEM((nf - 1, wrows, model), BF16),
            pltpu.VMEM((2, half, wrows, wide), BF16),
            pltpu.VMEM((half, wrows, wide), BF16),
            pltpu.VMEM((2, half - 1, wrows, wide), BF16),
            pltpu.SemaphoreType.DMA((pieces, 4)),
            pltpu.SemaphoreType.DMA((pieces, 4)),
            pltpu.SemaphoreType.DMA((nf - 1,)),
            pltpu.SemaphoreType.DMA((nf - 1,)),
            pltpu.SemaphoreType.DMA((nf - 1,)),
            pltpu.SemaphoreType.DMA((nf - 1,)),
            pltpu.SemaphoreType.DMA((2,)),
            pltpu.SemaphoreType.DMA((half - 1,)),
            pltpu.SemaphoreType.DMA((half - 1,)),
        ],
        compiler_params=pltpu.CompilerParams(
            collective_id=0, has_side_effects=True, vmem_limit_bytes=58 * 2**20
        ),
        cost_estimate=pl.CostEstimate(
            flops=10 * pair_flops, bytes_accessed=400 * 2**20, transcendentals=0
        ),
        name="fused",
    )(slopes, queries[0], keys[0], values[0], upstream[0], out_weight, wrow, wcol, mask)
    if wide > cut:
        weight_grad = lax.dynamic_slice_in_dim(weight_grad, me * cut % wide, cut, 1)
    return (dq[None], dk[None], dv[None], weight_grad)


def solution(mesh):
    in_specs = (
        P("fsdp", "ctx", None),
        P("fsdp", "ctx", None),
        P("fsdp", "ctx", None),
        P("fsdp", "ctx", None),
        P("fsdp", None),
        P(),
        P("fsdp", None),
        P("fsdp", None, "ctx"),
        P("fsdp", "ctx"),
    )
    out_specs = (
        P("fsdp", "ctx", None),
        P("fsdp", "ctx", None),
        P("fsdp", "ctx", None),
        P("fsdp", "ctx"),
    )
    return jax.shard_map(
        on_device, mesh=mesh, in_specs=in_specs, out_specs=out_specs, check_vma=False
    )
```

```python
import functools
import math

import jax
import jax.numpy as jnp
from jax import lax
from jax.experimental import pallas as pl
from jax.experimental.pallas import tpu as pltpu
from jax.sharding import PartitionSpec as P

BLOCK = 128
REACH = 2
GRID = 1024
FAR = 1e32
CHUNKS = 2
MESH = pl.DeviceIdType.MESH
F32 = jnp.float32
BF16 = jnp.bfloat16


def nt(a, b):
    return lax.dot_general(a, b, (((1,), (1,)), ((), ())), preferred_element_type=F32)


def nn(a, b):
    return lax.dot_general(a, b, (((1,), (0,)), ((), ())), preferred_element_type=F32)


def tn(a, b):
    return lax.dot_general(a, b, (((0,), (0,)), ((), ())), preferred_element_type=F32)


def greet(targets):
    barrier = pltpu.get_barrier_semaphore()
    for target in targets:
        pl.semaphore_signal(barrier, inc=1, device_id=target, device_id_type=MESH)
    pl.semaphore_wait(barrier, len(targets))


class Gather:
    def __init__(self, pieces, send_sem, recv_sem):
        n = lax.axis_size("ctx")
        me = lax.axis_index("ctx")
        self.parity = lax.rem(me, 2)
        self.up = lax.rem(me + 2, n)
        self.down = lax.rem(me + n - 2, n)
        self.partner = me + 1 - 2 * self.parity
        self.pieces = pieces
        self.send_sem = send_sem
        self.recv_sem = recv_sem

    def copy(self, i, slot):
        own, land = self.pieces[i]
        src = land(1 - self.parity) if slot == 3 else own
        target = (self.up, self.down, self.partner, self.partner)[slot]
        return pltpu.make_async_remote_copy(
            src_ref=src,
            dst_ref=land(slot),
            send_sem=self.send_sem.at[i, slot],
            recv_sem=self.recv_sem.at[i, slot],
            device_id={"ctx": target},
            device_id_type=MESH,
        )

    def start(self, pieces):
        for i in pieces:
            for slot in (0, 1, 2):
                self.copy(i, slot).start()

    def relay(self, i):
        src = 1 - self.parity
        own, land = self.pieces[i]
        pltpu.make_async_remote_copy(
            src_ref=own,
            dst_ref=land(src),
            send_sem=self.send_sem.at[i, 0],
            recv_sem=self.recv_sem.at[i, src],
            device_id={"ctx": self.partner},
            device_id_type=MESH,
        ).wait_recv()
        self.copy(i, 3).start()

    def arrived(self, slot, pieces):
        for i in pieces:
            own, land = self.pieces[i]
            pltpu.make_async_remote_copy(
                src_ref=own,
                dst_ref=land(slot),
                send_sem=self.send_sem.at[i, 0],
                recv_sem=self.recv_sem.at[i, slot],
                device_id={"ctx": self.partner},
                device_id_type=MESH,
            ).wait_recv()

    def sent(self):
        for i in range(len(self.pieces)):
            for slot in range(4):
                self.copy(i, slot).wait_send()


def remote(src, dst, send_sem, recv_sem, target):
    return pltpu.make_async_remote_copy(
        src_ref=src, dst_ref=dst, send_sem=send_sem, recv_sem=recv_sem, device_id=target, device_id_type=MESH
    )


def row_pieces(own_ref, land_ref, index, chunks):
    rows = own_ref.shape[0] // chunks

    def piece(j):
        span = pl.ds(j * rows, rows)

        def land(slot):
            return land_ref.at[slot, index, span] if index is not None else land_ref.at[slot, span]

        return (own_ref.at[span], land)

    return [piece(j) for j in range(chunks)]


def build_distance(far_ref, wrow_ref, wcol_ref, key_at, query_at, mask_row, tokens):
    qs = pl.ds(pl.multiple_of(query_at * tokens, BLOCK), tokens)
    qr = wrow_ref[0:1, qs]
    qg = wrow_ref[1:2, qs]
    for b in range(tokens // BLOCK):
        ks = pl.ds(pl.multiple_of(key_at * tokens + b * BLOCK, BLOCK), BLOCK)
        kc = wcol_ref[ks, :]
        dist = jnp.abs(kc[:, 0:1] - qr) + jnp.abs(kc[:, 1:2] - qg)
        far_ref[b * BLOCK : (b + 1) * BLOCK, :] = jnp.where(mask_row(b) > 0.5, dist, FAR)


def head_span(h, size):
    return pl.ds(pl.multiple_of(h * size, size), size)


def fused_kernel(
    heads,
    weight_scale,
    slopes_ref,
    q_ref,
    k_ref,
    v_ref,
    up_ref,
    w_ref,
    wrow_ref,
    wcol_ref,
    mask_ref,
    dq_ref,
    dk_ref,
    dv_ref,
    wg_ref,
    kv_ref,
    qbuf_ref,
    obuf_ref,
    sbuf_ref,
    og_ref,
    att_ref,
    stats_ref,
    wbuf_ref,
    far_ref,
    top_ref,
    total_ref,
    acc_ref,
    dka_ref,
    dva_ref,
    part_ref,
    pland_ref,
    wsum_ref,
    ysum_ref,
    zland_ref,
    send_sem,
    recv_sem,
    wsend_sem,
    wrecv_sem,
    gsend_sem,
    grecv_sem,
    ysem,
    zsend_sem,
    zrecv_sem,
):
    tokens, width = q_ref.shape
    size = width // heads
    blocks = tokens // BLOCK
    scaling = 1.0 / math.sqrt(size)
    n = lax.axis_size("ctx")
    nf = lax.axis_size("fsdp")
    me = lax.axis_index("ctx")
    fs = lax.axis_index("fsdp")
    wrows = w_ref.shape[0]
    model = up_ref.shape[1]
    half = n // 2
    wide = wsum_ref.shape[3]
    kv_pieces = range(0, 2 * CHUNKS)
    q_pieces = range(2 * CHUNKS, 3 * CHUNKS)
    o_pieces = range(3 * CHUNKS, 4 * CHUNKS)
    s_pieces = range(4 * CHUNKS, 4 * CHUNKS + 1)
    late_pieces = range(2 * CHUNKS, 4 * CHUNKS + 1)
    gather = Gather(
        row_pieces(k_ref, kv_ref, 0, CHUNKS)
        + row_pieces(v_ref, kv_ref, 1, CHUNKS)
        + row_pieces(q_ref, qbuf_ref, None, CHUNKS)
        + row_pieces(og_ref, obuf_ref, None, CHUNKS)
        + row_pieces(stats_ref, sbuf_ref, None, 1),
        send_sem,
        recv_sem,
    )
    parity = gather.parity
    near = 1 - 2 * parity
    home = REACH
    twin = fs + 1 - 2 * lax.rem(fs, 2)
    facing = lax.rem(fs + 2, nf)
    corner = lax.rem(twin + 2, nf)
    across = [{"ctx": lax.rem(me + 2 * d, n)} for d in range(1, half)]
    greet([{"ctx": gather.partner}] + across + [{"fsdp": twin}, {"fsdp": facing}])
    gather.start(kv_pieces)
    wcopies = [
        remote(
            wbuf_ref.at[1] if d == 2 else w_ref,
            wbuf_ref.at[d],
            wsend_sem.at[d],
            wrecv_sem.at[d],
            {"fsdp": facing if d == 1 else twin},
        )
        for d in range(3)
    ]
    wcopies[0].start()
    wcopies[1].start()

    top_ref[...] = jnp.full(top_ref.shape, -1e30, F32)
    total_ref[...] = jnp.zeros(total_ref.shape, F32)
    acc_ref[...] = jnp.zeros(acc_ref.shape, F32)

    def look(keys, values, offset):
        at = offset + REACH

        def mask_row(b):
            return mask_ref[pl.ds(at * blocks + b, 1), :]

        build_distance(far_ref, wrow_ref, wcol_ref, at, home, mask_row, tokens)

        @pl.loop(0, heads)
        def _(h):
            hs = head_span(h, size)
            s = nt(keys[:, hs], q_ref[:, hs]) * scaling - slopes_ref[h] * far_ref[...]
            old = top_ref[h]
            new = jnp.maximum(old, jnp.max(s, axis=0, keepdims=True))
            factor = jnp.exp(old - new)
            p = jnp.exp(s - new)
            top_ref[h] = new
            total_ref[h] = total_ref[h] * factor + jnp.sum(p, axis=0, keepdims=True)
            acc_ref[h] = acc_ref[h] * factor + tn(values[:, hs], p.astype(BF16))

    def look_slot(slot, offset):
        look(kv_ref.at[slot, 0], kv_ref.at[slot, 1], offset)

    def project(block, owner):
        cols = pl.ds(pl.multiple_of(owner * wrows, BLOCK), wrows)
        og_ref[:, cols] = nt(up_ref[...], block[...]).astype(BF16)

    look(k_ref, v_ref, 0)
    project(w_ref, fs)
    for i in kv_pieces:
        gather.relay(i)
        if i == CHUNKS - 1:
            gather.start(q_pieces)
    look_slot(1 - parity, 2 * near)
    wcopies[1].wait()
    wcopies[2].start()
    project(wbuf_ref.at[1], facing)
    wcopies[0].wait()
    project(wbuf_ref.at[0], twin)
    wcopies[2].wait()
    project(wbuf_ref.at[2], corner)
    gather.start(o_pieces)
    gather.arrived(2, kv_pieces)
    look_slot(2, near)
    gather.arrived(parity, kv_pieces)
    look_slot(parity, -2 * near)
    gather.arrived(3, kv_pieces)
    look_slot(3, -near)
    for h in range(heads):
        hs = slice(h * size, (h + 1) * size)
        total = total_ref[h]
        att = (acc_ref[h] / total).T.astype(BF16)
        att_ref[:, hs] = att
        stats_ref[h : h + 1, :] = top_ref[h] + jnp.log(total)
        prod = og_ref[:, hs].astype(F32) * att.astype(F32)
        stats_ref[heads + h : heads + h + 1, :] = jnp.sum(prod.T, axis=0, keepdims=True)
    stats_ref[2 * heads :, :] = mask_ref[...]
    gather.start(s_pieces)

    def part_of(owner):
        cols = pl.ds(pl.multiple_of(owner * wrows, BLOCK), wrows)
        return tn(att_ref[:, cols], up_ref[...])

    gcopies = [
        remote(
            part_ref.at[d],
            pland_ref.at[d],
            gsend_sem.at[d],
            grecv_sem.at[d],
            {"fsdp": facing if d == 2 else twin},
        )
        for d in range(3)
    ]
    part_ref[1] = part_of(corner).astype(BF16)
    gcopies[1].start()
    part_ref[0] = part_of(twin).astype(BF16)
    gcopies[0].start()

    def visit(keys, values, queries, grads, stats, key_at, query_at, to_query, to_key, first):
        def mask_row(b):
            return stats[pl.ds(2 * heads + (key_at - query_at + REACH) * blocks + b, 1), :]

        build_distance(far_ref, wrow_ref, wcol_ref, key_at, query_at, mask_row, tokens)

        @pl.loop(0, heads)
        def _(h):
            hs = head_span(h, size)
            k, q, g = keys[:, hs], queries[:, hs], grads[:, hs]
            s = nt(k, q) * scaling - slopes_ref[h] * far_ref[...]
            p = jnp.exp(s - stats[pl.ds(h, 1), :])
            ds = (p * (nt(values[:, hs], g) - stats[pl.ds(heads + h, 1), :])).astype(BF16)
            if to_query:
                part = tn(k, ds)
                acc_ref[h] = part if first else acc_ref[h] + part
            if to_key:
                kpart = nn(ds, q)
                vpart = nn(p.astype(BF16), g)
                dka_ref[h] = kpart if first else dka_ref[h] + kpart
                dva_ref[h] = vpart if first else dva_ref[h] + vpart

    def to_query(slot, offset):
        visit(
            kv_ref.at[slot, 0], kv_ref.at[slot, 1], q_ref, og_ref, stats_ref,
            home + offset, home, True, False, False,
        )

    def to_key(slot, offset):
        visit(
            k_ref, v_ref, qbuf_ref.at[slot], obuf_ref.at[slot], sbuf_ref.at[slot],
            home, home + offset, False, True, False,
        )

    for i in q_pieces:
        gather.relay(i)
    visit(k_ref, v_ref, q_ref, og_ref, stats_ref, home, home, True, True, True)
    gcopies[1].wait()
    part_ref[2] = (part_of(facing) + pland_ref[1].astype(F32)).astype(BF16)
    gcopies[2].start()
    to_query(0, -2)
    for i in o_pieces:
        gather.relay(i)
    to_query(1, 2)
    for i in s_pieces:
        gather.relay(i)
    to_query(2, near)
    to_query(3, -near)
    for h in range(heads):
        dq_ref[:, h * size : (h + 1) * size] = (acc_ref[h].T * scaling).astype(BF16)

    gcopies[0].wait()
    gcopies[2].wait()
    mine = part_of(fs) + pland_ref[0].astype(F32) + pland_ref[2].astype(F32)
    for c in range(n):
        at = c * (model // n) // wide * wide
        wsum_ref[c % 2, c // 2] = mine[:, at : at + wide].astype(BF16)
    ycopy = remote(
        wsum_ref.at[1 - parity], ysum_ref, ysem.at[0], ysem.at[1], {"ctx": gather.partner}
    )
    ycopy.start()

    to_key(1 - parity, 2 * near)
    gather.arrived(2, late_pieces)
    to_key(2, near)

    ycopy.wait()
    row = lax.div(me, 2)
    zcopies = []
    for d in range(half):
        k = lax.rem(row + d, half)
        pair_sum = wsum_ref[parity, k].astype(F32) + ysum_ref[k].astype(F32)
        if d == 0:
            wg_ref[...] = pair_sum
            continue
        zland_ref[0, d - 1] = pair_sum.astype(BF16)
        copy = remote(
            zland_ref.at[0, d - 1], zland_ref.at[1, d - 1], zsend_sem.at[d - 1], zrecv_sem.at[d - 1], across[d - 1]
        )
        copy.start()
        zcopies.append(copy)

    gather.arrived(parity, late_pieces)
    to_key(parity, -2 * near)
    gather.arrived(3, late_pieces)
    to_key(3, -near)
    for h in range(heads):
        hs = slice(h * size, (h + 1) * size)
        dk_ref[:, hs] = (dka_ref[h] * scaling).astype(BF16)
        dv_ref[:, hs] = dva_ref[h].astype(BF16)
    total = wg_ref[...]
    for d in range(1, half):
        zcopies[d - 1].wait()
        total = total + zland_ref[1, d - 1].astype(F32)
    wg_ref[...] = total * weight_scale
    gather.sent()


def on_device(
    queries, keys, values, upstream, out_weight, slopes, patch_index, pair_lists, pair_counts
):
    n = lax.axis_size("ctx")
    nf = lax.axis_size("fsdp")
    me = lax.axis_index("ctx")
    tokens, width = queries.shape[1:]
    model = upstream.shape[2]
    heads = slopes.shape[0]
    size = width // heads
    blocks = tokens // BLOCK
    window = 2 * REACH + 1
    slots = window * blocks
    mask_rows = -(-slots // 8) * 8

    positions = patch_index[0]
    around = lax.dynamic_slice_in_dim(
        jnp.concatenate([positions, positions]), lax.rem(me + n - REACH, n) * tokens, window * tokens
    )
    rows_cols = jnp.stack([around // GRID, around % GRID]).astype(F32)
    wrow = jnp.pad(rows_cols, ((0, 6), (0, 0)))
    wcol = wrow.T
    pairs = pair_lists[0]
    listed = jnp.arange(pairs.shape[1]) < pair_counts[0, 0]
    hit = (
        listed[None, None, :]
        & (pairs[0][None, None, :] == jnp.arange(blocks)[None, :, None])
        & (pairs[1][None, None, :] == jnp.arange(mask_rows)[:, None, None])
    )
    block_mask = jnp.any(hit, axis=2).astype(F32)
    mask = jnp.broadcast_to(block_mask[:, :, None], (mask_rows, blocks, BLOCK)).reshape(
        mask_rows, tokens
    )

    vmem = pl.BlockSpec(memory_space=pltpu.VMEM)
    smem = pl.BlockSpec(memory_space=pltpu.SMEM)
    block = jax.ShapeDtypeStruct((tokens, width), BF16)
    pair_flops = 2 * tokens * tokens * window * width
    stat_rows = 2 * heads + mask_rows
    pieces = 4 * CHUNKS + 1
    wrows = out_weight.shape[0]
    cut = model // n
    wide = max(cut, BLOCK)
    half = n // 2
    dq, dk, dv, weight_grad = pl.pallas_call(
        functools.partial(fused_kernel, heads, 1.0 / math.sqrt(tokens * n * nf)),
        out_shape=(block, block, block, jax.ShapeDtypeStruct((wrows, wide), F32)),
        in_specs=[smem] + [vmem] * 8,
        out_specs=(vmem,) * 4,
        scratch_shapes=[
            pltpu.VMEM((4, 2, tokens, width), BF16),
            pltpu.VMEM((4, tokens, width), BF16),
            pltpu.VMEM((4, tokens, width), BF16),
            pltpu.VMEM((4, stat_rows, tokens), F32),
            pltpu.VMEM((tokens, width), BF16),
            pltpu.VMEM((tokens, width), BF16),
            pltpu.VMEM((stat_rows, tokens), F32),
            pltpu.VMEM((3,) + out_weight.shape, BF16),
            pltpu.VMEM((tokens, tokens), F32),
            pltpu.VMEM((heads, 1, tokens), F32),
            pltpu.VMEM((heads, 1, tokens), F32),
            pltpu.VMEM((heads, size, tokens), F32),
            pltpu.VMEM((heads, tokens, size), F32),
            pltpu.VMEM((heads, tokens, size), F32),
            pltpu.VMEM((3, wrows, model), BF16),
            pltpu.VMEM((3, wrows, model), BF16),
            pltpu.VMEM((2, half, wrows, wide), BF16),
            pltpu.VMEM((half, wrows, wide), BF16),
            pltpu.VMEM((2, half - 1, wrows, wide), BF16),
            pltpu.SemaphoreType.DMA((pieces, 4)),
            pltpu.SemaphoreType.DMA((pieces, 4)),
            pltpu.SemaphoreType.DMA((3,)),
            pltpu.SemaphoreType.DMA((3,)),
            pltpu.SemaphoreType.DMA((3,)),
            pltpu.SemaphoreType.DMA((3,)),
            pltpu.SemaphoreType.DMA((2,)),
            pltpu.SemaphoreType.DMA((half - 1,)),
            pltpu.SemaphoreType.DMA((half - 1,)),
        ],
        compiler_params=pltpu.CompilerParams(
            collective_id=0, has_side_effects=True, vmem_limit_bytes=58 * 2**20
        ),
        cost_estimate=pl.CostEstimate(
            flops=10 * pair_flops, bytes_accessed=400 * 2**20, transcendentals=0
        ),
        name="fused",
    )(slopes, queries[0], keys[0], values[0], upstream[0], out_weight, wrow, wcol, mask)
    if wide > cut:
        weight_grad = lax.dynamic_slice_in_dim(weight_grad, me * cut % wide, cut, 1)
    return (dq[None], dk[None], dv[None], weight_grad)


def solution(mesh):
    in_specs = (
        P("fsdp", "ctx", None),
        P("fsdp", "ctx", None),
        P("fsdp", "ctx", None),
        P("fsdp", "ctx", None),
        P("fsdp", None),
        P(),
        P("fsdp", None),
        P("fsdp", None, "ctx"),
        P("fsdp", "ctx"),
    )
    out_specs = (
        P("fsdp", "ctx", None),
        P("fsdp", "ctx", None),
        P("fsdp", "ctx", None),
        P("fsdp", "ctx"),
    )
    return jax.shard_map(
        on_device, mesh=mesh, in_specs=in_specs, out_specs=out_specs, check_vma=False
    )
```
